32 devices in a mesh: row: 4 (over z), col: 8 (over y, x, core).
Axes of the slice: x: 2, y: 2, z: 4, core: 2. Of those that a mesh axis runs over, the one named last changes fastest.
Arguments:
- pair: bfloat16 [128, 128, 128], P('row', 'col'), may hold values from -6 to 6
- gain_in: float32 [128], replicated, may hold values from 0.1 to 1.9
- w_left_gate: bfloat16 [128, 128], replicated, may hold values from -0.5 to 0.5
- w_left: bfloat16 [128, 128], replicated, may hold values from -0.5 to 0.5
- w_right_gate: bfloat16 [128, 128], replicated, may hold values from -0.5 to 0.5
- w_right: bfloat16 [128, 128], replicated, may hold values from -0.5 to 0.5
- gain_out: float32 [128], replicated, may hold values from 0.1 to 1.9
- w_out_gate: bfloat16 [128, 128], replicated, may hold values from -0.5 to 0.5
- w_out: bfloat16 [128, 128], replicated, may hold values from -0.5 to 0.5
Outputs:
- update: bfloat16 [128, 128, 128], P('row', 'col')
The draws below stay inside these ranges and needn't reach their ends.
All inputs are finite; a program needn't handle non-finite values.
Results may differ from the reference program's by a relative error of at most 0.0081.
Values may be sent and summed in bfloat16 or wider, within the bound.
A program may use at most 64 MiB of HBM per device.

```python
import jax
import jax.numpy as jnp
from jax import lax

C = 128
H = 128
N = 128


def levels(stream_key, shape, cuts, low, high):
    def one(axis_at, blocks):
        draws = jax.random.uniform(jax.random.fold_in(jax.random.fold_in(stream_key, 6), axis_at), (blocks,), jnp.float32, low / len(cuts), high / len(cuts))
        return jnp.repeat(jnp.exp(draws), shape[axis_at] // blocks).reshape((-1,) + (1,) * (len(shape) - axis_at - 1))

    loudness = one(*cuts[0])
    for cut in cuts[1:]:
        loudness = loudness * one(*cut)
    return loudness


def gaussian(key, shape, spread, most, shards=(), kind=jnp.bfloat16):
    entries = spread * jax.random.normal(key, shape, jnp.float32)
    if shards:
        entries = entries * levels(key, shape, shards, -0.22, 0.18)
    return jnp.clip(entries, -most, most).astype(kind)


def setup_inputs(seed: int = 0) -> dict:
    arg_keys = jax.random.split(jax.random.key(seed), 10)
    return {
        "pair": gaussian(arg_keys[0], (N, N, C), 1.0, 6.0, ((0, 4), (1, 8))),
        "gain_in": jnp.clip(1.0 + 0.18 * jax.random.normal(arg_keys[1], (C,), jnp.float32), 0.1, 1.9),
        "w_left_gate": gaussian(arg_keys[2], (C, H), C ** -0.5, 0.5),
        "w_left": gaussian(arg_keys[3], (C, H), C ** -0.5, 0.5),
        "w_right_gate": gaussian(arg_keys[4], (C, H), C ** -0.5, 0.5),
        "w_right": gaussian(arg_keys[5], (C, H), C ** -0.5, 0.5),
        "gain_out": jnp.clip(1.0 + 0.18 * jax.random.normal(arg_keys[6], (H,), jnp.float32), 0.1, 1.9),
        "w_out_gate": gaussian(arg_keys[7], (C, C), C ** -0.5, 0.5),
        "w_out": gaussian(arg_keys[8], (H, C), H ** -0.5, 0.5),
    }


def layer_norm(values, gain):
    mean = lax.optimization_barrier(jnp.mean(values, axis=-1, keepdims=True))
    centred = values - mean
    variance = lax.optimization_barrier(jnp.mean(centred * centred, axis=-1, keepdims=True))
    return centred * jax.lax.rsqrt(variance + 1e-05) * gain

def project(normed, weight):
    return jnp.einsum('ijc,ch->ijh', normed.astype(jnp.float32), weight.astype(jnp.float32))

def reference(pair, gain_in, w_left_gate, w_left, w_right_gate, w_right, gain_out, w_out_gate, w_out):
    normed = layer_norm(pair.astype(jnp.float32), gain_in.astype(jnp.float32)).astype(jnp.bfloat16)
    left = (jax.nn.sigmoid(project(normed, w_left_gate)) * project(normed, w_left)).astype(jnp.bfloat16)
    right = (jax.nn.sigmoid(project(normed, w_right_gate)) * project(normed, w_right)).astype(jnp.bfloat16)
    mixed = jnp.einsum('ikh,jkh->ijh', left.astype(jnp.float32), right.astype(jnp.float32))
    out_normed = layer_norm(mixed, gain_out.astype(jnp.float32)).astype(jnp.bfloat16)
    gate = jax.nn.sigmoid(project(normed, w_out_gate))
    return (gate * project(out_normed, w_out)).astype(jnp.bfloat16)
```

```python
import functools

import jax
import jax.numpy as jnp
from jax import lax
from jax.experimental import pallas as pl
from jax.experimental.pallas import tpu as pltpu
from jax.sharding import PartitionSpec as P

MESH = pl.DeviceIdType.MESH
F32 = jnp.float32
BF16 = jnp.bfloat16
CORES = 2
PARTS = 2


def layer_norm(values, gain):
    mean = jnp.mean(values, axis=-1, keepdims=True)
    centred = values - mean
    variance = jnp.mean(centred * centred, axis=-1, keepdims=True)
    return centred * lax.rsqrt(variance + 1e-05) * gain


def gated(normed, w_gate, w):
    gate = jnp.dot(normed, w_gate, preferred_element_type=F32)
    value = jnp.dot(normed, w, preferred_element_type=F32)
    return (jax.nn.sigmoid(gate) * value).astype(BF16)


def kernel(
    nr, nc,
    pair, gain_in, w_left_gate, w_left, w_right_gate, w_right, gain_out, w_out_gate, w_out,
    out,
    pair_v, gain_in_v, w_right_gate_v, w_right_v, w_left_gate_v, w_left_v, w_out_gate_v, gain_out_v,
    w_out_v, load_sem,
    normed_f, normed_t, gate, chain, give, left, left_f, right_f, acc, mine, part, inbox,
    give_send, left_send, left_recv, up_send, down_send, far_send, chain_recv, part_send,
    inbox_recv,
):
    rows, cols, width = pair.shape
    chips = nc // CORES
    half = cols * cols
    part_j = cols // PARTS
    r = lax.axis_index("row")
    c = lax.axis_index("col")
    chip, core = c // CORES, c % CORES
    sibling = chip * CORES + 1 - core
    last = nr - 1

    loads = [
        pltpu.make_async_copy(source, target, load_sem.at[n])
        for n, (source, target) in enumerate((
            (pair, pair_v), (gain_in, gain_in_v), (w_right_gate, w_right_gate_v),
            (w_right, w_right_v), (w_left_gate, w_left_gate_v), (w_left, w_left_v),
            (w_out_gate, w_out_gate_v), (gain_out, gain_out_v), (w_out, w_out_v),
        ))
    ]
    for load in loads:
        load.start()

    barrier = pltpu.get_barrier_semaphore()

    def greet(row, col):
        pl.semaphore_signal(barrier, inc=1, device_id={"row": row, "col": col}, device_id_type=MESH)

    greet(r, sibling)
    for s in range(1, chips):
        greet(r, (chip + s) % chips * CORES + core)

    @pl.when(r > 0)
    def _():
        greet(r - 1, c)

    @pl.when(r < last)
    def _():
        greet(r + 1, c)

    @pl.when(r == 0)
    def _():
        greet(last, c)

    greeted = (
        chips + (r > 0).astype(jnp.int32) + (r < last).astype(jnp.int32) + (r == last).astype(jnp.int32)
    )

    def chain_copy(block, kc, jc, row, sem):
        piece = chain.at[block, kc, jc]
        return pltpu.make_async_remote_copy(
            src_ref=piece, dst_ref=piece, send_sem=sem.at[block, kc, jc],
            recv_sem=chain_recv.at[block, kc, jc],
            device_id={"row": row, "col": c}, device_id_type=MESH,
        )

    def far_copy(kc, jc):
        piece = chain.at[last, kc, jc]
        return pltpu.make_async_remote_copy(
            src_ref=piece, dst_ref=piece, send_sem=far_send.at[kc, jc],
            recv_sem=chain_recv.at[last, kc, jc],
            device_id={"row": 0, "col": c}, device_id_type=MESH,
        )

    def give_copy(jc):
        return pltpu.make_async_remote_copy(
            src_ref=give.at[jc], dst_ref=chain.at[r, core, jc], send_sem=give_send.at[jc],
            recv_sem=chain_recv.at[r, core, jc],
            device_id={"row": r, "col": sibling}, device_id_type=MESH,
        )

    def left_copy(kc):
        return pltpu.make_async_remote_copy(
            src_ref=left.at[kc], dst_ref=left.at[kc], send_sem=left_send, recv_sem=left_recv,
            device_id={"row": r, "col": sibling}, device_id_type=MESH,
        )

    def part_copy(block, jc, col, source):
        return pltpu.make_async_remote_copy(
            src_ref=part.at[block, jc], dst_ref=inbox.at[source, jc],
            send_sem=part_send.at[block, jc], recv_sem=inbox_recv.at[source, jc],
            device_id={"row": r, "col": col}, device_id_type=MESH,
        )

    def send_on(block, kc, jc, up, down):
        @pl.when(up)
        def _():
            chain_copy(block, kc, jc, r + 1, up_send).start()

        @pl.when(down)
        def _():
            chain_copy(block, kc, jc, r - 1, down_send).start()

    def goes_down(block):
        return jnp.logical_and(r > 0, jnp.logical_not(jnp.logical_and(block == last, r == 1)))

    def send_own(kc, jc):
        @pl.when(r == last)
        def _():
            far_copy(kc, jc).start()

        send_on(r, kc, jc, r < last, goes_down(r))

    for load in loads[:2]:
        load.wait()
    normed_f[...] = layer_norm(pair_v[...].reshape(rows * cols, width).astype(F32), gain_in_v[...])
    for load in loads[2:]:
        load.wait()

    def right_of(t):
        normed = normed_f[pl.ds(pl.multiple_of(t * half, half), half), :].astype(BF16)
        return gated(normed, w_right_gate_v[...], w_right_v[...]).reshape(PARTS, part_j, cols, width)

    chain[r, core] = right_of(core)
    pl.semaphore_wait(barrier, greeted)
    for jc in range(PARTS):
        send_own(core, jc)
    give[...] = right_of(1 - core)
    for jc in range(PARTS):
        give_copy(jc).start()

    for k in range(cols):
        normed_t[pl.ds(k * rows, rows), :] = normed_f[pl.ds(k, rows, stride=cols), :].astype(BF16)
    projected = gated(normed_t[...], w_left_gate_v[...], w_left_v[...]).reshape(cols, rows, width)
    left[core] = projected
    left_copy(core).start()
    left_f[core] = projected.astype(F32)

    def receive(block, kc, jc):
        chain_copy(block, kc, jc, r, up_send).wait_recv()

    for jc in range(PARTS):
        receive(r, 1 - core, jc)
        send_own(1 - core, jc)
    gate[...] = jax.nn.sigmoid(jnp.dot(normed_t[...], w_out_gate_v[...], preferred_element_type=F32))

    def mix(block, kc, jc, first):
        right_f[...] = chain[block, kc, jc].astype(F32)
        sums = [None if first else acc[jc, n] for n in range(part_j)]
        for k in range(cols):
            other = left_f[kc, k]
            for n in range(part_j):
                term = right_f[n, pl.ds(k, 1), :] * other
                sums[n] = term if sums[n] is None else sums[n] + term
        for n in range(part_j):
            acc[jc, n] = sums[n]

    def dispatch(block, jc):
        @pl.when(block == chip)
        def _():
            mine[jc] = acc[jc]

        @pl.when(block != chip)
        def _():
            part[block, jc] = acc[jc].astype(BF16)
            part_copy(block, jc, block * CORES + core, chip).start()

    for jc in range(PARTS):
        mix(r, core, jc, True)
    left_copy(1 - core).wait_recv()
    left_f[1 - core] = left[1 - core].astype(F32)
    for jc in range(PARTS):
        mix(r, 1 - core, jc, False)
        dispatch(r, jc)

    for step in range(1, nr):
        below = step <= r
        block = jnp.where(below, r - step, step)
        up = jnp.logical_and(below, r < last)
        down = jnp.logical_and(jnp.logical_not(below), goes_down(block))
        for first, kc in ((True, core), (False, 1 - core)):
            for jc in range(PARTS):
                receive(block, kc, jc)
                send_on(block, kc, jc, up, down)
                mix(block, kc, jc, first)
                if not first:
                    dispatch(block, jc)

    total = mine[...]
    for s in range(1, chips):
        source = (chip + s) % chips
        for jc in range(PARTS):
            part_copy(0, jc, sibling, source).wait_recv()
        total = total + inbox[source].astype(F32)
    out_normed = layer_norm(total.reshape(cols * rows, width), gain_out_v[...]).astype(BF16)
    normed_f[...] = gate[...] * jnp.dot(out_normed, w_out_v[...], preferred_element_type=F32)
    for i in range(rows):
        out[i] = normed_f[pl.ds(i, cols, stride=rows), :].astype(BF16)

    left_copy(core).wait_send()
    for jc in range(PARTS):
        give_copy(jc).wait_send()
        for block in range(nr):
            @pl.when(block != chip)
            def _(block=block):
                part_copy(block, jc, sibling, 0).wait_send()

            for kc in range(CORES):
                @pl.when(jnp.logical_and(r >= block, r < last))
                def _(block=block, kc=kc):
                    chain_copy(block, kc, jc, r + 1, up_send).wait_send()

                @pl.when(jnp.logical_and(r <= block, goes_down(block)))
                def _(block=block, kc=kc):
                    chain_copy(block, kc, jc, r - 1, down_send).wait_send()

        for kc in range(CORES):
            @pl.when(r == last)
            def _(kc=kc):
                far_copy(kc, jc).wait_send()


def solution(mesh):
    nr, nc = mesh.shape["row"], mesh.shape["col"]
    chips = nc // CORES
    assert chips == nr

    def per_device(
        pair, gain_in, w_left_gate, w_left, w_right_gate, w_right, gain_out, w_out_gate, w_out
    ):
        rows, cols, width = pair.shape
        assert rows == CORES * cols
        flat = rows * cols
        part_j = cols // PARTS
        dma = pltpu.SemaphoreType.DMA
        return pl.pallas_call(
            functools.partial(kernel, nr, nc),
            out_shape=jax.ShapeDtypeStruct(pair.shape, BF16),
            in_specs=[pl.BlockSpec(memory_space=pl.ANY)] * 9,
            out_specs=pl.BlockSpec(memory_space=pltpu.VMEM),
            scratch_shapes=[
                pltpu.VMEM((rows, cols, width), BF16),
                pltpu.VMEM((1, width), F32),
                *[pltpu.VMEM((width, width), BF16) for _ in range(5)],
                pltpu.VMEM((1, width), F32),
                pltpu.VMEM((width, width), BF16),
                dma((9,)),
                pltpu.VMEM((flat, width), F32),
                pltpu.VMEM((flat, width), BF16),
                pltpu.VMEM((flat, width), F32),
                pltpu.VMEM((nr, CORES, PARTS, part_j, cols, width), BF16),
                pltpu.VMEM((PARTS, part_j, cols, width), BF16),
                pltpu.VMEM((CORES, cols, rows, width), BF16),
                pltpu.VMEM((CORES, cols, rows, width), F32),
                pltpu.VMEM((part_j, cols, width), F32),
                pltpu.VMEM((PARTS, part_j, rows, width), F32),
                pltpu.VMEM((PARTS, part_j, rows, width), F32),
                pltpu.VMEM((nr, PARTS, part_j, rows, width), BF16),
                pltpu.VMEM((chips, PARTS, part_j, rows, width), BF16),
                dma((PARTS,)), dma, dma,
                dma((nr, CORES, PARTS)), dma((nr, CORES, PARTS)), dma((CORES, PARTS)),
                dma((nr, CORES, PARTS)), dma((nr, PARTS)), dma((chips, PARTS)),
            ],
            compiler_params=pltpu.CompilerParams(collective_id=0, has_side_effects=True),
        )(
            pair, gain_in.reshape(1, -1), w_left_gate, w_left, w_right_gate, w_right,
            gain_out.reshape(1, -1), w_out_gate, w_out,
        )

    return jax.shard_map(
        per_device,
        mesh=mesh,
        in_specs=(P("row", "col", None), P(), P(), P(), P(), P(), P(), P(), P()),
        out_specs=P("row", "col", None),
        check_vma=False,
    )
```

```python
import functools

import jax
import jax.numpy as jnp
from jax import lax
from jax.experimental import pallas as pl
from jax.experimental.pallas import tpu as pltpu
from jax.sharding import PartitionSpec as P

MESH = pl.DeviceIdType.MESH
F32 = jnp.float32
BF16 = jnp.bfloat16
CORES = 2
PARTS = 2


def layer_norm(values, gain):
    mean = jnp.mean(values, axis=-1, keepdims=True)
    centred = values - mean
    variance = jnp.mean(centred * centred, axis=-1, keepdims=True)
    return centred * lax.rsqrt(variance + 1e-05) * gain


def gated(normed, w_gate, w):
    gate = jnp.dot(normed, w_gate, preferred_element_type=F32)
    value = jnp.dot(normed, w, preferred_element_type=F32)
    return (jax.nn.sigmoid(gate) * value).astype(BF16)


def kernel(
    nr, nc,
    pair, gain_in, w_left_gate, w_left, w_right_gate, w_right, gain_out, w_out_gate, w_out,
    out,
    pair_v, gain_in_v, w_right_gate_v, w_right_v, w_left_gate_v, w_left_v, w_out_gate_v, gain_out_v,
    w_out_v, load_sem,
    normed_f, normed_t, gate, chain, give, left, left_f, right_f, acc, mine, part, inbox,
    give_send, left_send, left_recv, up_send, down_send, far_send, chain_recv, part_send,
    inbox_recv,
):
    rows, cols, width = pair.shape
    chips = nc // CORES
    half = cols * cols
    part_j = cols // PARTS
    r = lax.axis_index("row")
    c = lax.axis_index("col")
    chip, core = c // CORES, c % CORES
    sibling = chip * CORES + 1 - core
    last = nr - 1

    loads = [
        pltpu.make_async_copy(source, target, load_sem.at[n])
        for n, (source, target) in enumerate((
            (pair, pair_v), (gain_in, gain_in_v), (w_right_gate, w_right_gate_v),
            (w_right, w_right_v), (w_left_gate, w_left_gate_v), (w_left, w_left_v),
            (w_out_gate, w_out_gate_v), (gain_out, gain_out_v), (w_out, w_out_v),
        ))
    ]
    for load in loads:
        load.start()

    barrier = pltpu.get_barrier_semaphore()

    def greet(row, col):
        pl.semaphore_signal(barrier, inc=1, device_id={"row": row, "col": col}, device_id_type=MESH)

    greet(r, sibling)
    for s in range(1, chips):
        greet(r, (chip + s) % chips * CORES + core)

    @pl.when(r > 0)
    def _():
        greet(r - 1, c)

    @pl.when(r < last)
    def _():
        greet(r + 1, c)

    @pl.when(r == 0)
    def _():
        greet(last, c)

    greeted = (
        chips + (r > 0).astype(jnp.int32) + (r < last).astype(jnp.int32) + (r == last).astype(jnp.int32)
    )

    def chain_copy(block, kc, jc, row, sem):
        piece = chain.at[block, kc, jc]
        return pltpu.make_async_remote_copy(
            src_ref=piece, dst_ref=piece, send_sem=sem.at[block, kc, jc],
            recv_sem=chain_recv.at[block, kc, jc],
            device_id={"row": row, "col": c}, device_id_type=MESH,
        )

    def far_copy(kc, jc):
        piece = chain.at[last, kc, jc]
        return pltpu.make_async_remote_copy(
            src_ref=piece, dst_ref=piece, send_sem=far_send.at[kc, jc],
            recv_sem=chain_recv.at[last, kc, jc],
            device_id={"row": 0, "col": c}, device_id_type=MESH,
        )

    def give_copy(jc):
        return pltpu.make_async_remote_copy(
            src_ref=give.at[jc], dst_ref=chain.at[r, core, jc], send_sem=give_send.at[jc],
            recv_sem=chain_recv.at[r, core, jc],
            device_id={"row": r, "col": sibling}, device_id_type=MESH,
        )

    def left_copy(kc):
        return pltpu.make_async_remote_copy(
            src_ref=left.at[kc], dst_ref=left.at[kc], send_sem=left_send, recv_sem=left_recv,
            device_id={"row": r, "col": sibling}, device_id_type=MESH,
        )

    def part_copy(block, jc, col, source):
        return pltpu.make_async_remote_copy(
            src_ref=part.at[block, jc], dst_ref=inbox.at[source, jc],
            send_sem=part_send.at[block, jc], recv_sem=inbox_recv.at[source, jc],
            device_id={"row": r, "col": col}, device_id_type=MESH,
        )

    def send_on(block, kc, jc, up, down):
        @pl.when(up)
        def _():
            chain_copy(block, kc, jc, r + 1, up_send).start()

        @pl.when(down)
        def _():
            chain_copy(block, kc, jc, r - 1, down_send).start()

    def goes_down(block):
        return jnp.logical_and(r > 0, jnp.logical_not(jnp.logical_and(block == last, r == 1)))

    def send_own(kc, jc):
        @pl.when(r == last)
        def _():
            far_copy(kc, jc).start()

        send_on(r, kc, jc, r < last, goes_down(r))

    for load in loads[:2]:
        load.wait()
    normed_f[...] = layer_norm(pair_v[...].reshape(rows * cols, width).astype(F32), gain_in_v[...])
    for load in loads[2:]:
        load.wait()

    def right_of(t):
        normed = normed_f[pl.ds(pl.multiple_of(t * half, half), half), :].astype(BF16)
        return gated(normed, w_right_gate_v[...], w_right_v[...]).reshape(PARTS, part_j, cols, width)

    chain[r, core] = right_of(core)
    pl.semaphore_wait(barrier, greeted)
    for jc in range(PARTS):
        send_own(core, jc)
    give[...] = right_of(1 - core)
    for jc in range(PARTS):
        give_copy(jc).start()

    for k in range(cols):
        normed_t[pl.ds(k * rows, rows), :] = normed_f[pl.ds(k, rows, stride=cols), :].astype(BF16)
    projected = gated(normed_t[...], w_left_gate_v[...], w_left_v[...]).reshape(cols, rows, width)
    left[core] = projected
    left_copy(core).start()
    left_f[core] = projected.astype(F32)

    def receive(block, kc, jc):
        chain_copy(block, kc, jc, r, up_send).wait_recv()

    for jc in range(PARTS):
        receive(r, 1 - core, jc)
        send_own(1 - core, jc)
    gate[...] = jax.nn.sigmoid(jnp.dot(normed_t[...], w_out_gate_v[...], preferred_element_type=F32))

    def mix(block, kc, jc, first):
        right_f[...] = chain[block, kc, jc].astype(F32)
        sums = [None if first else acc[jc, n] for n in range(part_j)]
        for k in range(cols):
            other = left_f[kc, k]
            for n in range(part_j):
                term = right_f[n, pl.ds(k, 1), :] * other
                sums[n] = term if sums[n] is None else sums[n] + term
        for n in range(part_j):
            acc[jc, n] = sums[n]

    def dispatch(block, jc):
        @pl.when(block == chip)
        def _():
            mine[jc] = acc[jc]

        @pl.when(block != chip)
        def _():
            part[block, jc] = acc[jc].astype(BF16)
            part_copy(block, jc, block * CORES + core, chip).start()

    for jc in range(PARTS):
        mix(r, core, jc, True)
    left_copy(1 - core).wait_recv()
    left_f[1 - core] = left[1 - core].astype(F32)
    for jc in range(PARTS):
        mix(r, 1 - core, jc, False)
        dispatch(r, jc)

    fewer = jnp.minimum(r, last - r)
    for step in range(1, nr):
        paired = step <= 2 * fewer
        below = jnp.where(paired, step % 2 == 1, r > last - r)
        distance = jnp.where(paired, (step + 1) // 2, step - fewer)
        block = jnp.where(below, r - distance, r + distance)
        up = jnp.logical_and(below, r < last)
        down = jnp.logical_and(jnp.logical_not(below), goes_down(block))
        for first, kc in ((True, core), (False, 1 - core)):
            for jc in range(PARTS):
                receive(block, kc, jc)
                send_on(block, kc, jc, up, down)
                mix(block, kc, jc, first)
                if not first:
                    dispatch(block, jc)

    total = mine[...]
    for s in range(1, chips):
        source = (chip + s) % chips
        for jc in range(PARTS):
            part_copy(0, jc, sibling, source).wait_recv()
        total = total + inbox[source].astype(F32)
    out_normed = layer_norm(total.reshape(cols * rows, width), gain_out_v[...]).astype(BF16)
    normed_f[...] = gate[...] * jnp.dot(out_normed, w_out_v[...], preferred_element_type=F32)
    for i in range(rows):
        out[i] = normed_f[pl.ds(i, cols, stride=rows), :].astype(BF16)

    left_copy(core).wait_send()
    for jc in range(PARTS):
        give_copy(jc).wait_send()
        for block in range(nr):
            @pl.when(block != chip)
            def _(block=block):
                part_copy(block, jc, sibling, 0).wait_send()

            for kc in range(CORES):
                @pl.when(jnp.logical_and(r >= block, r < last))
                def _(block=block, kc=kc):
                    chain_copy(block, kc, jc, r + 1, up_send).wait_send()

                @pl.when(jnp.logical_and(r <= block, goes_down(block)))
                def _(block=block, kc=kc):
                    chain_copy(block, kc, jc, r - 1, down_send).wait_send()

        for kc in range(CORES):
            @pl.when(r == last)
            def _(kc=kc):
                far_copy(kc, jc).wait_send()


def solution(mesh):
    nr, nc = mesh.shape["row"], mesh.shape["col"]
    chips = nc // CORES
    assert chips == nr

    def per_device(
        pair, gain_in, w_left_gate, w_left, w_right_gate, w_right, gain_out, w_out_gate, w_out
    ):
        rows, cols, width = pair.shape
        assert rows == CORES * cols
        flat = rows * cols
        part_j = cols // PARTS
        dma = pltpu.SemaphoreType.DMA
        return pl.pallas_call(
            functools.partial(kernel, nr, nc),
            out_shape=jax.ShapeDtypeStruct(pair.shape, BF16),
            in_specs=[pl.BlockSpec(memory_space=pl.ANY)] * 9,
            out_specs=pl.BlockSpec(memory_space=pltpu.VMEM),
            scratch_shapes=[
                pltpu.VMEM((rows, cols, width), BF16),
                pltpu.VMEM((1, width), F32),
                *[pltpu.VMEM((width, width), BF16) for _ in range(5)],
                pltpu.VMEM((1, width), F32),
                pltpu.VMEM((width, width), BF16),
                dma((9,)),
                pltpu.VMEM((flat, width), F32),
                pltpu.VMEM((flat, width), BF16),
                pltpu.VMEM((flat, width), F32),
                pltpu.VMEM((nr, CORES, PARTS, part_j, cols, width), BF16),
                pltpu.VMEM((PARTS, part_j, cols, width), BF16),
                pltpu.VMEM((CORES, cols, rows, width), BF16),
                pltpu.VMEM((CORES, cols, rows, width), F32),
                pltpu.VMEM((part_j, cols, width), F32),
                pltpu.VMEM((PARTS, part_j, rows, width), F32),
                pltpu.VMEM((PARTS, part_j, rows, width), F32),
                pltpu.VMEM((nr, PARTS, part_j, rows, width), BF16),
                pltpu.VMEM((chips, PARTS, part_j, rows, width), BF16),
                dma((PARTS,)), dma, dma,
                dma((nr, CORES, PARTS)), dma((nr, CORES, PARTS)), dma((CORES, PARTS)),
                dma((nr, CORES, PARTS)), dma((nr, PARTS)), dma((chips, PARTS)),
            ],
            compiler_params=pltpu.CompilerParams(collective_id=0, has_side_effects=True, vmem_limit_bytes=24 * 2**20),
        )(
            *(
                pltpu.with_memory_space_constraint(operand, pltpu.HBM)
                for operand in (
                    pair, gain_in.reshape(1, -1), w_left_gate, w_left, w_right_gate, w_right,
                    gain_out.reshape(1, -1), w_out_gate, w_out,
                )
            )
        )

    return jax.shard_map(
        per_device,
        mesh=mesh,
        in_specs=(P("row", "col", None), P(), P(), P(), P(), P(), P(), P(), P()),
        out_specs=P("row", "col", None),
        check_vma=False,
    )
```

```python
import functools

import jax
import jax.numpy as jnp
from jax import lax
from jax.experimental import pallas as pl
from jax.experimental.pallas import tpu as pltpu
from jax.sharding import PartitionSpec as P

MESH = pl.DeviceIdType.MESH
F32 = jnp.float32
BF16 = jnp.bfloat16
CORES = 2
PARTS = 2


def layer_norm(values, gain):
    mean = jnp.mean(values, axis=-1, keepdims=True)
    centred = values - mean
    variance = jnp.mean(centred * centred, axis=-1, keepdims=True)
    return centred * lax.rsqrt(variance + 1e-05) * gain


def gated(normed, w_gate, w):
    gate = jnp.dot(normed, w_gate, preferred_element_type=F32)
    value = jnp.dot(normed, w, preferred_element_type=F32)
    return (jax.nn.sigmoid(gate) * value).astype(BF16)


def kernel(
    nr, nc,
    pair, gain_in, w_left_gate, w_left, w_right_gate, w_right, gain_out, w_out_gate, w_out,
    out,
    pair_v, gain_in_v, w_right_gate_v, w_right_v, w_left_gate_v, w_left_v, w_out_gate_v, gain_out_v,
    w_out_v, load_sem,
    normed_f, normed_t, gate, chain, give, left, left_f, right_f, acc, mine, part, inbox,
    give_send, left_send, left_recv, up_send, down_send, far_send, chain_recv, corner_in, part_send,
    inbox_recv,
):
    rows, cols, width = pair.shape
    chips = nc // CORES
    half = cols * cols
    part_j = cols // PARTS
    r = lax.axis_index("row")
    c = lax.axis_index("col")
    chip, core = c // CORES, c % CORES
    sibling = chip * CORES + 1 - core
    last = nr - 1
    square = chips == 4
    chip_x, chip_y = chip % 2, chip // 2
    across_x = (chip_y * 2 + 1 - chip_x) * CORES + core
    across_y = ((1 - chip_y) * 2 + chip_x) * CORES + core

    loads = [
        pltpu.make_async_copy(source, target, load_sem.at[n])
        for n, (source, target) in enumerate((
            (pair, pair_v), (gain_in, gain_in_v), (w_right_gate, w_right_gate_v),
            (w_right, w_right_v), (w_left_gate, w_left_gate_v), (w_left, w_left_v),
            (w_out_gate, w_out_gate_v), (gain_out, gain_out_v), (w_out, w_out_v),
        ))
    ]
    for load in loads:
        load.start()

    barrier = pltpu.get_barrier_semaphore()

    def greet(row, col):
        pl.semaphore_signal(barrier, inc=1, device_id={"row": row, "col": col}, device_id_type=MESH)

    greet(r, sibling)
    if square:
        greet(r, across_x)
        greet(r, across_y)
    else:
        for s in range(1, chips):
            greet(r, (chip + s) % chips * CORES + core)

    @pl.when(r > 0)
    def _():
        greet(r - 1, c)

    @pl.when(r < last)
    def _():
        greet(r + 1, c)

    @pl.when(r == 0)
    def _():
        greet(last, c)

    greeted = (
        (3 if square else chips) + (r > 0).astype(jnp.int32) + (r < last).astype(jnp.int32) + (r == last).astype(jnp.int32)
    )

    def chain_copy(block, kc, jc, row, sem):
        piece = chain.at[block, kc, jc]
        return pltpu.make_async_remote_copy(
            src_ref=piece, dst_ref=piece, send_sem=sem.at[block, kc, jc],
            recv_sem=chain_recv.at[block, kc, jc],
            device_id={"row": row, "col": c}, device_id_type=MESH,
        )

    def far_copy(kc, jc):
        piece = chain.at[last, kc, jc]
        return pltpu.make_async_remote_copy(
            src_ref=piece, dst_ref=piece, send_sem=far_send.at[kc, jc],
            recv_sem=chain_recv.at[last, kc, jc],
            device_id={"row": 0, "col": c}, device_id_type=MESH,
        )

    def give_copy(jc):
        return pltpu.make_async_remote_copy(
            src_ref=give.at[jc], dst_ref=chain.at[r, core, jc], send_sem=give_send.at[jc],
            recv_sem=chain_recv.at[r, core, jc],
            device_id={"row": r, "col": sibling}, device_id_type=MESH,
        )

    def left_copy(kc):
        return pltpu.make_async_remote_copy(
            src_ref=left.at[kc], dst_ref=left.at[kc], send_sem=left_send, recv_sem=left_recv,
            device_id={"row": r, "col": sibling}, device_id_type=MESH,
        )

    def part_copy(block, jc, col, source):
        return pltpu.make_async_remote_copy(
            src_ref=part.at[block, jc], dst_ref=inbox.at[source, jc],
            send_sem=part_send.at[block, jc], recv_sem=inbox_recv.at[source, jc],
            device_id={"row": r, "col": col}, device_id_type=MESH,
        )

    def send_on(block, kc, jc, up, down):
        @pl.when(up)
        def _():
            chain_copy(block, kc, jc, r + 1, up_send).start()

        @pl.when(down)
        def _():
            chain_copy(block, kc, jc, r - 1, down_send).start()

    def goes_down(block):
        return jnp.logical_and(r > 0, jnp.logical_not(jnp.logical_and(block == last, r == 1)))

    def send_own(kc, jc):
        @pl.when(r == last)
        def _():
            far_copy(kc, jc).start()

        send_on(r, kc, jc, r < last, goes_down(r))

    for load in loads[:2]:
        load.wait()
    normed_f[...] = layer_norm(pair_v[...].reshape(rows * cols, width).astype(F32), gain_in_v[...])
    for load in loads[2:]:
        load.wait()

    def right_of(t):
        normed = normed_f[pl.ds(pl.multiple_of(t * half, half), half), :].astype(BF16)
        return gated(normed, w_right_gate_v[...], w_right_v[...]).reshape(PARTS, part_j, cols, width)

    chain[r, core] = right_of(core)
    pl.semaphore_wait(barrier, greeted)
    for jc in range(PARTS):
        send_own(core, jc)
    if square:
        pl.semaphore_signal(
            corner_in, inc=1, device_id={"row": r, "col": across_x}, device_id_type=MESH
        )
    give[...] = right_of(1 - core)
    for jc in range(PARTS):
        give_copy(jc).start()

    for k in range(cols):
        normed_t[pl.ds(k * rows, rows), :] = normed_f[pl.ds(k, rows, stride=cols), :].astype(BF16)
    projected = gated(normed_t[...], w_left_gate_v[...], w_left_v[...]).reshape(cols, rows, width)
    left[core] = projected
    left_copy(core).start()
    left_f[core] = projected.astype(F32)

    def receive(block, kc, jc):
        chain_copy(block, kc, jc, r, up_send).wait_recv()

    for jc in range(PARTS):
        receive(r, 1 - core, jc)
        send_own(1 - core, jc)
    gate[...] = jax.nn.sigmoid(jnp.dot(normed_t[...], w_out_gate_v[...], preferred_element_type=F32))

    def mix(block, kc, jc, first):
        right_f[...] = chain[block, kc, jc].astype(F32)
        sums = [None if first else acc[jc, n] for n in range(part_j)]
        for k in range(cols):
            other = left_f[kc, k]
            for n in range(part_j):
                term = right_f[n, pl.ds(k, 1), :] * other
                sums[n] = term if sums[n] is None else sums[n] + term
        for n in range(part_j):
            acc[jc, n] = sums[n]

    def dispatch(block, jc):
        @pl.when(block == chip)
        def _():
            mine[jc] = acc[jc]

        @pl.when(block != chip)
        def _():
            part[block, jc] = acc[jc].astype(BF16)
            part_copy(block, jc, block * CORES + core, chip).start()

    if square:
        pl.semaphore_wait(corner_in, 1)
    for jc in range(PARTS):
        mix(r, core, jc, True)
    left_copy(1 - core).wait_recv()
    left_f[1 - core] = left[1 - core].astype(F32)
    for jc in range(PARTS):
        mix(r, 1 - core, jc, False)
        dispatch(r, jc)

    fewer = jnp.minimum(r, last - r)
    for step in range(1, nr):
        paired = step <= 2 * fewer
        below = jnp.where(paired, step % 2 == 1, r > last - r)
        distance = jnp.where(paired, (step + 1) // 2, step - fewer)
        block = jnp.where(below, r - distance, r + distance)
        up = jnp.logical_and(below, r < last)
        down = jnp.logical_and(jnp.logical_not(below), goes_down(block))
        for jc in range(PARTS):
            for first, kc in ((True, core), (False, 1 - core)):
                receive(block, kc, jc)
                send_on(block, kc, jc, up, down)
                mix(block, kc, jc, first)
            dispatch(block, jc)

    part_rows = part_j * rows
    for jc in range(PARTS):
        total = mine[jc]
        for s in range(1, chips):
            source = (chip + s) % chips
            part_copy(0, jc, sibling, source).wait_recv()
            total = total + inbox[source, jc].astype(F32)
        out_normed = layer_norm(total.reshape(part_rows, width), gain_out_v[...]).astype(BF16)
        here = pl.ds(jc * part_rows, part_rows)
        normed_f[here, :] = gate[here, :] * jnp.dot(
            out_normed, w_out_v[...], preferred_element_type=F32
        )
    for i in range(rows):
        out[i] = normed_f[pl.ds(i, cols, stride=rows), :].astype(BF16)

    left_copy(core).wait_send()
    for jc in range(PARTS):
        give_copy(jc).wait_send()
        for block in range(nr):
            @pl.when(block != chip)
            def _(block=block):
                part_copy(block, jc, sibling, 0).wait_send()

            for kc in range(CORES):
                @pl.when(jnp.logical_and(r >= block, r < last))
                def _(block=block, kc=kc):
                    chain_copy(block, kc, jc, r + 1, up_send).wait_send()

                @pl.when(jnp.logical_and(r <= block, goes_down(block)))
                def _(block=block, kc=kc):
                    chain_copy(block, kc, jc, r - 1, down_send).wait_send()

        for kc in range(CORES):
            @pl.when(r == last)
            def _(kc=kc):
                far_copy(kc, jc).wait_send()


def solution(mesh):
    nr, nc = mesh.shape["row"], mesh.shape["col"]
    chips = nc // CORES
    assert chips == nr

    def per_device(
        pair, gain_in, w_left_gate, w_left, w_right_gate, w_right, gain_out, w_out_gate, w_out
    ):
        rows, cols, width = pair.shape
        assert rows == CORES * cols
        flat = rows * cols
        part_j = cols // PARTS
        dma = pltpu.SemaphoreType.DMA
        return pl.pallas_call(
            functools.partial(kernel, nr, nc),
            out_shape=jax.ShapeDtypeStruct(pair.shape, BF16),
            in_specs=[pl.BlockSpec(memory_space=pl.ANY)] * 9,
            out_specs=pl.BlockSpec(memory_space=pltpu.VMEM),
            scratch_shapes=[
                pltpu.VMEM((rows, cols, width), BF16),
                pltpu.VMEM((1, width), F32),
                *[pltpu.VMEM((width, width), BF16) for _ in range(5)],
                pltpu.VMEM((1, width), F32),
                pltpu.VMEM((width, width), BF16),
                dma((9,)),
                pltpu.VMEM((flat, width), F32),
                pltpu.VMEM((flat, width), BF16),
                pltpu.VMEM((flat, width), F32),
                pltpu.VMEM((nr, CORES, PARTS, part_j, cols, width), BF16),
                pltpu.VMEM((PARTS, part_j, cols, width), BF16),
                pltpu.VMEM((CORES, cols, rows, width), BF16),
                pltpu.VMEM((CORES, cols, rows, width), F32),
                pltpu.VMEM((part_j, cols, width), F32),
                pltpu.VMEM((PARTS, part_j, rows, width), F32),
                pltpu.VMEM((PARTS, part_j, rows, width), F32),
                pltpu.VMEM((nr, PARTS, part_j, rows, width), BF16),
                pltpu.VMEM((chips, PARTS, part_j, rows, width), BF16),
                dma((PARTS,)), dma, dma,
                dma((nr, CORES, PARTS)), dma((nr, CORES, PARTS)), dma((CORES, PARTS)),
                dma((nr, CORES, PARTS)), pltpu.SemaphoreType.REGULAR, dma((nr, PARTS)),
                dma((chips, PARTS)),
            ],
            compiler_params=pltpu.CompilerParams(collective_id=0, has_side_effects=True, vmem_limit_bytes=24 * 2**20),
        )(
            *(
                pltpu.with_memory_space_constraint(operand, pltpu.HBM)
                for operand in (
                    pair, gain_in.reshape(1, -1), w_left_gate, w_left, w_right_gate, w_right,
                    gain_out.reshape(1, -1), w_out_gate, w_out,
                )
            )
        )

    return jax.shard_map(
        per_device,
        mesh=mesh,
        in_specs=(P("row", "col", None), P(), P(), P(), P(), P(), P(), P(), P()),
        out_specs=P("row", "col", None),
        check_vma=False,
    )
```

```python
import functools

import jax
import jax.numpy as jnp
from jax import lax
from jax.experimental import pallas as pl
from jax.experimental.pallas import tpu as pltpu
from jax.sharding import PartitionSpec as P

MESH = pl.DeviceIdType.MESH
F32 = jnp.float32
BF16 = jnp.bfloat16
CORES = 2
PARTS = 2


def layer_norm(values, gain):
    mean = jnp.mean(values, axis=-1, keepdims=True)
    centred = values - mean
    variance = jnp.mean(centred * centred, axis=-1, keepdims=True)
    return centred * lax.rsqrt(variance + 1e-05) * gain


def gated(normed, w_gate, w):
    gate = jnp.dot(normed, w_gate, preferred_element_type=F32)
    value = jnp.dot(normed, w, preferred_element_type=F32)
    return (jax.nn.sigmoid(gate) * value).astype(BF16)


def kernel(
    nr, nc,
    pair, gain_in, w_left_gate, w_left, w_right_gate, w_right, gain_out, w_out_gate, w_out,
    out,
    pair_v, gain_in_v, w_right_gate_v, w_right_v, w_left_gate_v, w_left_v, w_out_gate_v, gain_out_v,
    w_out_v, load_sem,
    normed_f, normed_t, gate, chain, give, left, left_f, right_f, acc, mine, part, inbox,
    give_send, left_send, left_recv, up_send, down_send, far_send, chain_recv, corner_in, part_send,
    inbox_recv,
):
    rows, cols, width = pair.shape
    chips = nc // CORES
    half = cols * cols
    part_j = cols // PARTS
    r = lax.axis_index("row")
    c = lax.axis_index("col")
    chip, core = c // CORES, c % CORES
    sibling = chip * CORES + 1 - core
    last = nr - 1
    square = chips == 4
    chip_x, chip_y = chip % 2, chip // 2
    across_x = (chip_y * 2 + 1 - chip_x) * CORES + core
    across_y = ((1 - chip_y) * 2 + chip_x) * CORES + core

    loads = [
        pltpu.make_async_copy(source, target, load_sem.at[n])
        for n, (source, target) in enumerate((
            (pair, pair_v), (gain_in, gain_in_v), (w_right_gate, w_right_gate_v),
            (w_right, w_right_v), (w_left_gate, w_left_gate_v), (w_left, w_left_v),
            (w_out_gate, w_out_gate_v), (gain_out, gain_out_v), (w_out, w_out_v),
        ))
    ]
    for load in loads[:4]:
        load.start()

    barrier = pltpu.get_barrier_semaphore()

    def greet(row, col):
        pl.semaphore_signal(barrier, inc=1, device_id={"row": row, "col": col}, device_id_type=MESH)

    greet(r, sibling)
    if square:
        greet(r, across_x)
        greet(r, across_y)
    else:
        for s in range(1, chips):
            greet(r, (chip + s) % chips * CORES + core)

    @pl.when(r > 0)
    def _():
        greet(r - 1, c)

    @pl.when(r < last)
    def _():
        greet(r + 1, c)

    @pl.when(r == 0)
    def _():
        greet(last, c)

    for load in loads[4:]:
        load.start()

    greeted = (
        (3 if square else chips) + (r > 0).astype(jnp.int32) + (r < last).astype(jnp.int32) + (r == last).astype(jnp.int32)
    )

    def chain_copy(block, kc, jc, row, sem):
        piece = chain.at[block, kc, jc]
        return pltpu.make_async_remote_copy(
            src_ref=piece, dst_ref=piece, send_sem=sem.at[block, kc, jc],
            recv_sem=chain_recv.at[block, kc, jc],
            device_id={"row": row, "col": c}, device_id_type=MESH,
        )

    def far_copy(kc, jc):
        piece = chain.at[last, kc, jc]
        return pltpu.make_async_remote_copy(
            src_ref=piece, dst_ref=piece, send_sem=far_send.at[kc, jc],
            recv_sem=chain_recv.at[last, kc, jc],
            device_id={"row": 0, "col": c}, device_id_type=MESH,
        )

    def give_copy(jc):
        return pltpu.make_async_remote_copy(
            src_ref=give.at[jc], dst_ref=chain.at[r, core, jc], send_sem=give_send.at[jc],
            recv_sem=chain_recv.at[r, core, jc],
            device_id={"row": r, "col": sibling}, device_id_type=MESH,
        )

    def left_copy(kc):
        return pltpu.make_async_remote_copy(
            src_ref=left.at[kc], dst_ref=left.at[kc], send_sem=left_send, recv_sem=left_recv,
            device_id={"row": r, "col": sibling}, device_id_type=MESH,
        )

    def part_copy(block, jc, col, source):
        return pltpu.make_async_remote_copy(
            src_ref=part.at[block, jc], dst_ref=inbox.at[source, jc],
            send_sem=part_send.at[block, jc], recv_sem=inbox_recv.at[source, jc],
            device_id={"row": r, "col": col}, device_id_type=MESH,
        )

    def send_on(block, kc, jc, up, down):
        @pl.when(up)
        def _():
            chain_copy(block, kc, jc, r + 1, up_send).start()

        @pl.when(down)
        def _():
            chain_copy(block, kc, jc, r - 1, down_send).start()

    def goes_down(block):
        return jnp.logical_and(r > 0, jnp.logical_not(jnp.logical_and(block == last, r == 1)))

    def send_own(kc, jc):
        @pl.when(r == last)
        def _():
            far_copy(kc, jc).start()

        send_on(r, kc, jc, r < last, goes_down(r))

    for load in loads[:2]:
        load.wait()
    normed_f[...] = layer_norm(pair_v[...].reshape(rows * cols, width).astype(F32), gain_in_v[...])
    for load in loads[2:4]:
        load.wait()

    def right_of(t):
        normed = normed_f[pl.ds(pl.multiple_of(t * half, half), half), :].astype(BF16)
        return gated(normed, w_right_gate_v[...], w_right_v[...]).reshape(PARTS, part_j, cols, width)

    chain[r, core] = right_of(core)
    pl.semaphore_wait(barrier, greeted)
    for jc in range(PARTS):
        send_own(core, jc)
    if square:
        pl.semaphore_signal(
            corner_in, inc=1, device_id={"row": r, "col": across_x}, device_id_type=MESH
        )
    give[...] = right_of(1 - core)
    for jc in range(PARTS):
        give_copy(jc).start()

    for load in loads[4:]:
        load.wait()
    for k in range(cols):
        normed_t[pl.ds(k * rows, rows), :] = normed_f[pl.ds(k, rows, stride=cols), :].astype(BF16)
    projected = gated(normed_t[...], w_left_gate_v[...], w_left_v[...]).reshape(cols, rows, width)
    left[core] = projected
    left_copy(core).start()
    left_f[core] = projected.astype(F32)

    def receive(block, kc, jc):
        chain_copy(block, kc, jc, r, up_send).wait_recv()

    for jc in range(PARTS):
        receive(r, 1 - core, jc)
        send_own(1 - core, jc)
    gate[...] = jax.nn.sigmoid(jnp.dot(normed_t[...], w_out_gate_v[...], preferred_element_type=F32))

    def mix(block, kc, jc, first):
        right_f[...] = chain[block, kc, jc].astype(F32)
        sums = [None if first else acc[jc, n] for n in range(part_j)]
        for k in range(cols):
            other = left_f[kc, k]
            for n in range(part_j):
                term = right_f[n, pl.ds(k, 1), :] * other
                sums[n] = term if sums[n] is None else sums[n] + term
        for n in range(part_j):
            acc[jc, n] = sums[n]

    def dispatch(block, jc):
        @pl.when(block == chip)
        def _():
            mine[jc] = acc[jc]

        @pl.when(block != chip)
        def _():
            part[block, jc] = acc[jc].astype(BF16)
            part_copy(block, jc, block * CORES + core, chip).start()

    if square:
        pl.semaphore_wait(corner_in, 1)
    for jc in range(PARTS):
        mix(r, core, jc, True)
    left_copy(1 - core).wait_recv()
    left_f[1 - core] = left[1 - core].astype(F32)
    for jc in range(PARTS):
        mix(r, 1 - core, jc, False)
        dispatch(r, jc)

    fewer = jnp.minimum(r, last - r)

    def taken(step):
        paired = step <= 2 * fewer
        below = jnp.where(paired, step % 2 == 1, r > last - r)
        distance = jnp.where(paired, (step + 1) // 2, step - fewer)
        if step >= nr - 2:
            distance = jnp.where(r == 0, 2 * nr - 3 - step, distance)
        block = jnp.where(below, r - distance, r + distance)
        up = jnp.logical_and(below, r < last)
        down = jnp.logical_and(jnp.logical_not(below), goes_down(block))
        return block, below, up, down

    passed = None
    for step in range(1, nr):
        block, below, up, down = taken(step)
        ahead = None
        if 1 < step < nr - 1:
            later, later_below, later_up, _ = taken(step + 1)
            ahead = jnp.logical_and(later_up, jnp.logical_not(below))
        for jc in range(PARTS):
            for first, kc in ((True, core), (False, 1 - core)):
                def take(block=block, kc=kc, jc=jc, up=up, down=down):
                    receive(block, kc, jc)
                    send_on(block, kc, jc, up, down)

                if passed is None:
                    take()
                else:
                    pl.when(jnp.logical_not(passed))(take)
                if ahead is not None:
                    @pl.when(ahead)
                    def _(later=later, kc=kc, jc=jc):
                        receive(later, kc, jc)
                        chain_copy(later, kc, jc, r + 1, up_send).start()

                mix(block, kc, jc, first)
            dispatch(block, jc)
        passed = ahead

    part_rows = part_j * rows
    for jc in range(PARTS):
        total = mine[jc]
        for s in range(1, chips):
            source = (chip + s) % chips
            part_copy(0, jc, sibling, source).wait_recv()
            total = total + inbox[source, jc].astype(F32)
        out_normed = layer_norm(total.reshape(part_rows, width), gain_out_v[...]).astype(BF16)
        here = pl.ds(jc * part_rows, part_rows)
        normed_f[here, :] = gate[here, :] * jnp.dot(
            out_normed, w_out_v[...], preferred_element_type=F32
        )
    for i in range(rows):
        out[i] = normed_f[pl.ds(i, cols, stride=rows), :].astype(BF16)

    left_copy(core).wait_send()
    for jc in range(PARTS):
        give_copy(jc).wait_send()
        for block in range(nr):
            @pl.when(block != chip)
            def _(block=block):
                part_copy(block, jc, sibling, 0).wait_send()

            for kc in range(CORES):
                @pl.when(jnp.logical_and(r >= block, r < last))
                def _(block=block, kc=kc):
                    chain_copy(block, kc, jc, r + 1, up_send).wait_send()

                @pl.when(jnp.logical_and(r <= block, goes_down(block)))
                def _(block=block, kc=kc):
                    chain_copy(block, kc, jc, r - 1, down_send).wait_send()

        for kc in range(CORES):
            @pl.when(r == last)
            def _(kc=kc):
                far_copy(kc, jc).wait_send()


def solution(mesh):
    nr, nc = mesh.shape["row"], mesh.shape["col"]
    chips = nc // CORES
    assert chips == nr

    def per_device(
        pair, gain_in, w_left_gate, w_left, w_right_gate, w_right, gain_out, w_out_gate, w_out
    ):
        rows, cols, width = pair.shape
        assert rows == CORES * cols
        flat = rows * cols
        part_j = cols // PARTS
        dma = pltpu.SemaphoreType.DMA
        return pl.pallas_call(
            functools.partial(kernel, nr, nc),
            out_shape=jax.ShapeDtypeStruct(pair.shape, BF16),
            in_specs=[pl.BlockSpec(memory_space=pl.ANY)] * 9,
            out_specs=pl.BlockSpec(memory_space=pltpu.VMEM),
            scratch_shapes=[
                pltpu.VMEM((rows, cols, width), BF16),
                pltpu.VMEM((1, width), F32),
                *[pltpu.VMEM((width, width), BF16) for _ in range(5)],
                pltpu.VMEM((1, width), F32),
                pltpu.VMEM((width, width), BF16),
                dma((9,)),
                pltpu.VMEM((flat, width), F32),
                pltpu.VMEM((flat, width), BF16),
                pltpu.VMEM((flat, width), F32),
                pltpu.VMEM((nr, CORES, PARTS, part_j, cols, width), BF16),
                pltpu.VMEM((PARTS, part_j, cols, width), BF16),
                pltpu.VMEM((CORES, cols, rows, width), BF16),
                pltpu.VMEM((CORES, cols, rows, width), F32),
                pltpu.VMEM((part_j, cols, width), F32),
                pltpu.VMEM((PARTS, part_j, rows, width), F32),
                pltpu.VMEM((PARTS, part_j, rows, width), F32),
                pltpu.VMEM((nr, PARTS, part_j, rows, width), BF16),
                pltpu.VMEM((chips, PARTS, part_j, rows, width), BF16),
                dma((PARTS,)), dma, dma,
                dma((nr, CORES, PARTS)), dma((nr, CORES, PARTS)), dma((CORES, PARTS)),
                dma((nr, CORES, PARTS)), pltpu.SemaphoreType.REGULAR, dma((nr, PARTS)),
                dma((chips, PARTS)),
            ],
            compiler_params=pltpu.CompilerParams(collective_id=0, has_side_effects=True, vmem_limit_bytes=24 * 2**20),
        )(
            *(
                pltpu.with_memory_space_constraint(operand, pltpu.HBM)
                for operand in (
                    pair, gain_in.reshape(1, -1), w_left_gate, w_left, w_right_gate, w_right,
                    gain_out.reshape(1, -1), w_out_gate, w_out,
                )
            )
        )

    return jax.shard_map(
        per_device,
        mesh=mesh,
        in_specs=(P("row", "col", None), P(), P(), P(), P(), P(), P(), P(), P()),
        out_specs=P("row", "col", None),
        check_vma=False,
    )
```
